512 devices in a mesh: ctx: 32 (over z_hi, x, core), ch: 16 (over z_lo, y).
Axes of the slice: x: 4, y: 4, z: 16 (z_hi: 4, z_lo: 4; z = z_hi * 4 + z_lo), core: 2. Of those that a mesh axis runs over, the one named last changes fastest.
Arguments:
- inputs: bfloat16 [16384, 2048], P('ctx', 'ch'), may hold values from -6 to 6
- gate_in: bfloat16 [16384, 2048], P('ctx', 'ch'), may hold values from -6 to 6
- kernel: bfloat16 [16384, 2048], P('ctx', 'ch'), may hold values from -0.046875 to 0.046875
- skip_gain: float32 [2048], P('ch'), may hold values from 0.5 to 1.5
- out_weight: bfloat16 [2048, 2048], P(None, 'ch'), may hold values from -0.125 to 0.125
Outputs:
- output: bfloat16 [16384, 2048], P('ctx', 'ch')
The draws below stay inside these ranges and needn't reach their ends.
All inputs are finite; a program needn't handle non-finite values.
Results may differ from the reference program's by a relative error of at most 0.0058.
Values may be sent and summed in bfloat16 or wider, within the bound.
No kernel may reach another device: no remote copies, remote signals or barrier semaphores. Data moves between devices by JAX's collectives and lax.ppermute only.
A program may use at most 64 MiB of HBM per device.

```python
import math
import jax
import jax.numpy as jnp
from jax import lax

C = 2048
BLOCK = 128
SEQ = 16384


def levels(own_key, extent, split, least, high):
    def one(position, shards_of):
        draws = jax.random.uniform(jax.random.fold_in(jax.random.fold_in(own_key, 6), position), (shards_of,), jnp.float32, least / len(split), high / len(split))
        return jnp.repeat(jnp.exp(draws), extent[position] // shards_of).reshape((-1,) + (1,) * (len(extent) - position - 1))

    gain = one(*split[0])
    for cut in split[1:]:
        gain = gain * one(*cut)
    return gain


def noise(key, extent, width, most, split=(), dtype=jnp.bfloat16):
    drawn = jax.random.normal(key, extent, jnp.float32) * width
    if len(split) > 0:
        drawn = levels(key, extent, split, -0.22, 0.18) * drawn
    return jnp.clip(drawn, min=-most, max=most).astype(dtype)


def setup_inputs(seed: int = 0) -> dict:
    key_list = jax.random.split(jax.random.key(seed), 6)
    inputs = noise(key_list[0], (SEQ, C), 1.0, 6.0, ((0, 32), (1, 16)))
    gate_in = noise(key_list[1], (SEQ, C), 1.0, 6.0, ((0, 32), (1, 16)))
    kernel = noise(key_list[2], (SEQ, C), SEQ ** -0.5, 0.046875, ((0, 32), (1, 16)))
    skip_gain = jnp.clip(0.5 + 1.0 * jax.random.uniform(key_list[3], (C,), jnp.float32) ** levels(key_list[3], (C,), ((0, 16),), -0.2, 0.2), 0.5, 1.5)
    out_weight = noise(key_list[4], (C, C), C ** -0.5, 0.125, ((1, 16),))
    return {"inputs": inputs, "gate_in": gate_in, "kernel": kernel, "skip_gain": skip_gain, "out_weight": out_weight}


def tables(half_len):
    rows_idx = lax.broadcasted_iota(jnp.int32, (2 * half_len, half_len), 0)
    time_index = lax.broadcasted_iota(jnp.int32, (2 * half_len, half_len), 1)
    frequency = jnp.where(rows_idx < half_len, rows_idx, rows_idx - half_len)
    angles = ((frequency * time_index) % (2 * half_len)).astype(jnp.float32) * (math.pi / half_len)
    nyquist = jnp.where(time_index % 2 == 0, 1.0, -1.0).astype(jnp.float32)
    forward = jnp.where(rows_idx < half_len, jnp.cos(angles), jnp.where(rows_idx == half_len, nyquist, -jnp.sin(angles)))
    forward = forward.astype(jnp.bfloat16)
    time_out = lax.broadcasted_iota(jnp.int32, (2 * half_len, 2 * half_len), 0)
    packed_col = lax.broadcasted_iota(jnp.int32, (2 * half_len, 2 * half_len), 1)
    freq_out = jnp.where(packed_col < half_len, packed_col, packed_col - half_len)
    angles_out = ((freq_out * time_out) % (2 * half_len)).astype(jnp.float32) * (math.pi / half_len)
    sign_out = jnp.where(time_out % 2 == 0, 1.0, -1.0).astype(jnp.float32)
    inverse = jnp.where(packed_col == 0, 1.0, jnp.where(packed_col < half_len, 2.0 * jnp.cos(angles_out), jnp.where(packed_col == half_len, sign_out, -2.0 * jnp.sin(angles_out))))
    inverse = (inverse / (2.0 * half_len)).astype(jnp.float32)
    return forward, inverse


def spectra_of(raw_rows, forward):
    half_len = forward.shape[1]
    blocks = raw_rows.reshape(raw_rows.shape[0] // half_len, half_len, raw_rows.shape[1])
    spectra = jnp.einsum("ft,ntc->nfc", forward.astype(jnp.float32), blocks.astype(jnp.float32))
    rounded = spectra.astype(jnp.bfloat16)
    return lax.optimization_barrier(rounded).astype(jnp.float32)


def block_convolve(first_seq, second_seq):
    count = first_seq.shape[0]
    spectrum = jnp.fft.fft(first_seq, n=2 * count, axis=0) * jnp.fft.fft(second_seq, n=2 * count, axis=0)
    return jnp.fft.ifft(spectrum, axis=0)[:count]


def block_products(left, right):
    half_len = left.shape[1] // 2
    lowest = lax.broadcasted_iota(jnp.int32, (1, half_len, 1), 1) == 0
    left_complex = lax.complex(left[:, :half_len], jnp.where(lowest, 0.0, left[:, half_len:]))
    right_complex = lax.complex(right[:, :half_len], jnp.where(lowest, 0.0, right[:, half_len:]))
    combined = block_convolve(left_complex, right_complex)
    highest = block_convolve(left[:, half_len], right[:, half_len]).real
    real_part = combined.real
    imag_part = jnp.where(lowest, highest[:, None, :], combined.imag)
    return jnp.concatenate([real_part, imag_part], axis=1)


def reference(inputs, gate_in, kernel, skip_gain, out_weight):
    forward, inverse = tables(BLOCK)
    group = min(C, 256)
    pieces = []
    for begin in range(0, C, group):
        input_spectra = spectra_of(inputs[:, begin:begin + group], forward)
        kernel_spectra = spectra_of(kernel[:, begin:begin + group], forward)
        pieces.append(block_products(input_spectra, kernel_spectra))
    spectral_sum = jnp.concatenate(pieces, axis=2)
    prior_sum = jnp.concatenate([jnp.zeros_like(spectral_sum[:1]), spectral_sum[:-1]], axis=0)
    from_here = jnp.einsum("tf,nfc->ntc", inverse[:BLOCK], spectral_sum, precision=lax.Precision.HIGHEST)
    from_prior = jnp.einsum("tf,nfc->ntc", inverse[BLOCK:], prior_sum, precision=lax.Precision.HIGHEST)
    convolved = (from_here + from_prior).reshape(SEQ, C)
    gated = ((convolved + skip_gain[None, :] * inputs.astype(jnp.float32)) * jax.nn.silu(gate_in.astype(jnp.float32))).astype(jnp.bfloat16)
    return jnp.dot(gated, out_weight, preferred_element_type=jnp.float32).astype(jnp.bfloat16)
```

```python
import jax
import jax.numpy as jnp
from jax import lax
from jax.experimental import pallas as pl
from jax.experimental.pallas import tpu as pltpu
from jax.sharding import Mesh, PartitionSpec as P

BLOCK = 128
CTX = ("zh", "x", "core")
CH = ("zl", "y")
NCH = 4
CHUNK = 16


def iota(shape, dim):
    return lax.broadcasted_iota(jnp.int32, shape, dim)


def one_hot(index_of_row, size):
    rows, cols = iota((size, size), 0), iota((size, size), 1)
    return jnp.where(index_of_row(rows) == cols, 1.0, 0.0).astype(jnp.bfloat16)


def prep_kernel(x_ref, k_ref, g_ref, xk_ref, gt_ref):
    place = one_hot(lambda r: (r & 3) * BLOCK + (r >> 2), 512)

    def channel_rows(ref):
        wide = jnp.concatenate([ref[b * BLOCK : (b + 1) * BLOCK, :] for b in range(4)], axis=1)
        turned = lax.dot_general(
            place, wide, (((1,), (1,)), ((), ())), preferred_element_type=jnp.float32
        )
        return turned.astype(jnp.bfloat16).reshape(32, 16, BLOCK)

    xk_ref[:, :16, :] = channel_rows(x_ref)
    xk_ref[:, 16:, :] = channel_rows(k_ref)
    gt_ref[...] = channel_rows(g_ref)


def conv_kernel(skip_ref, xk_ref, g_ref, o_ref, xpad, krow, gate, tt, acc, ys):
    sort = one_hot(lambda r: ((r >> 2) & 31) * 16 + (r >> 7) * 4 + (r & 3), 512)

    def by_channel(rows):
        return jnp.dot(sort, rows, preferred_element_type=jnp.float32)

    xs_all = by_channel(xk_ref[:, :16, :].reshape(512, BLOCK))
    for c in range(NCH):
        xpad[c, :BLOCK, :] = jnp.zeros((BLOCK, BLOCK), jnp.float32)
        xpad[c, BLOCK:, :] = xs_all[c * BLOCK : (c + 1) * BLOCK, :]
    krow[...] = by_channel(xk_ref[:, 16:, :].reshape(512, BLOCK))
    gate[...] = by_channel(g_ref[...].reshape(512, BLOCK))
    upper = iota((BLOCK, BLOCK), 1) >= iota((BLOCK, BLOCK), 0)

    def channel(c, carry):
        before = jnp.zeros((BLOCK, BLOCK), jnp.float32)
        for first in range(0, BLOCK, CHUNK):
            pieces = []
            for j in range(CHUNK):
                m = first + j
                row = jnp.broadcast_to(krow[pl.ds(c * BLOCK + m, 1), :], (BLOCK, BLOCK))
                turned = pltpu.roll(row, 0, 1, stride=1, stride_axis=0)
                tt[j * BLOCK : (j + 1) * BLOCK, :] = jnp.where(upper, turned, before).astype(
                    jnp.bfloat16
                )
                before = turned
                pieces.append(
                    xpad[c, BLOCK - m + first : 2 * BLOCK - m, :].astype(jnp.bfloat16)
                )
            product = jnp.dot(
                jnp.concatenate(pieces, axis=1), tt[...], preferred_element_type=jnp.float32
            )
            if first == 0:
                acc[...] = product
            else:
                acc[first:, :] += product
        base = pl.multiple_of(c * BLOCK, BLOCK)
        v = gate[pl.ds(base, BLOCK), :]
        mixed = acc[...] + skip_ref[c] * xpad[c, BLOCK:, :]
        ys[pl.ds(base, BLOCK), :] = (mixed * (v / (1.0 + jnp.exp(-v)))).astype(jnp.bfloat16)
        return carry

    lax.fori_loop(0, NCH, channel, 0)
    back = one_hot(lambda r: (r & 3) * BLOCK + (r >> 2), 512)
    o_ref[...] = jnp.dot(back, ys[...], preferred_element_type=jnp.float32).astype(jnp.bfloat16)


def mix_kernel(y_ref, g_ref, w0_ref, w1_ref, w2_ref, w3_ref, o_ref):
    sort = one_hot(lambda r: ((r >> 2) & 31) * 16 + (r >> 7) * 4 + (r & 3), 512)
    rows = jnp.dot(sort, g_ref[...], preferred_element_type=jnp.float32).astype(jnp.bfloat16)
    for shift, w_ref in enumerate((w0_ref, w1_ref, w2_ref, w3_ref)):
        owner = (y_ref[0] + 4 - shift) & 3
        for z in range(4):
            o_ref[z * 4 + owner] = lax.dot_general(
                rows, w_ref[z], (((0,), (0,)), ((), ())), preferred_element_type=jnp.float32
            ).astype(jnp.bfloat16)


VMEM = pl.BlockSpec(memory_space=pltpu.VMEM)
SMEM = pl.BlockSpec(memory_space=pltpu.SMEM)


def shards(inputs, gate_in, kernel, skip_gain, out_weight):
    bf16 = jnp.bfloat16
    xk, gt = pl.pallas_call(
        prep_kernel,
        out_shape=(
            jax.ShapeDtypeStruct((32, 32, BLOCK), bf16),
            jax.ShapeDtypeStruct((32, 16, BLOCK), bf16),
        ),
        in_specs=[VMEM] * 3,
        out_specs=(VMEM, VMEM),
    )(inputs, kernel, gate_in)
    xk = lax.all_to_all(xk, CTX, 0, 0, tiled=True)
    gt = lax.all_to_all(gt, CTX, 0, 0, tiled=True)

    w_rows = lax.all_to_all(out_weight.reshape(4, 512, BLOCK), "zl", 0, 0, tiled=True)
    w_parts = [w_rows] + [
        lax.ppermute(w_rows, "y", [(i, (i + shift) % 4) for i in range(4)]) for shift in (1, 2, 3)
    ]

    skip = lax.dynamic_slice(skip_gain, (lax.axis_index(CTX) * NCH,), (NCH,))
    gated = pl.pallas_call(
        conv_kernel,
        out_shape=jax.ShapeDtypeStruct((512, BLOCK), bf16),
        in_specs=[SMEM, VMEM, VMEM],
        out_specs=VMEM,
        scratch_shapes=[
            pltpu.VMEM((NCH, 2 * BLOCK, BLOCK), jnp.float32),
            pltpu.VMEM((512, BLOCK), jnp.float32),
            pltpu.VMEM((512, BLOCK), jnp.float32),
            pltpu.VMEM((CHUNK * BLOCK, BLOCK), bf16),
            pltpu.VMEM((BLOCK, BLOCK), jnp.float32),
            pltpu.VMEM((512, BLOCK), bf16),
        ],
    )(skip, xk, gt)
    gated = lax.all_to_all(gated, CTX + ("y",), 0, 0, tiled=True)

    partial = pl.pallas_call(
        mix_kernel,
        out_shape=jax.ShapeDtypeStruct((16, BLOCK, BLOCK), bf16),
        in_specs=[SMEM] + [VMEM] * 5,
        out_specs=VMEM,
    )(lax.axis_index("y").reshape(1), gated, *w_parts)
    partial = lax.all_to_all(partial, CH, 0, 0, tiled=True)
    total = jnp.sum(partial.reshape(4, 512, BLOCK).astype(jnp.float32), axis=0)
    return total.astype(bf16)


def solution(mesh):
    fine = Mesh(mesh.devices.reshape(4, 4, 2, 4, 4), CTX + CH)
    placed = (P(CTX, CH), P(CTX, CH), P(CTX, CH), P(CH), P(None, CH))
    return jax.shard_map(
        shards, mesh=fine, in_specs=placed, out_specs=P(CTX, CH), check_vma=False
    )
```

```python
import jax
import jax.numpy as jnp
from jax import lax
from jax.experimental import pallas as pl
from jax.experimental.pallas import tpu as pltpu
from jax.sharding import Mesh, PartitionSpec as P

BLOCK = 128
CTX = ("zh", "x", "core")
CH = ("zl", "y")
NCH = 4
CHUNK = 16


def iota(shape, dim):
    return lax.broadcasted_iota(jnp.int32, shape, dim)


def one_hot(index_of_row, size):
    rows, cols = iota((size, size), 0), iota((size, size), 1)
    return jnp.where(index_of_row(rows) == cols, 1.0, 0.0).astype(jnp.bfloat16)


def prep_kernel(y_ref, x_ref, k_ref, w_ref, xk_ref, w0_ref, w1_ref, w2_ref, w3_ref):
    place = one_hot(lambda r: (r & 3) * BLOCK + (r >> 2), 512)

    def channel_rows(ref):
        wide = jnp.concatenate([ref[b * BLOCK : (b + 1) * BLOCK, :] for b in range(4)], axis=1)
        turned = lax.dot_general(
            place, wide, (((1,), (1,)), ((), ())), preferred_element_type=jnp.float32
        )
        return turned.astype(jnp.bfloat16).reshape(32, 16, BLOCK)

    xk_ref[:, :16, :] = channel_rows(x_ref)
    xk_ref[:, 16:, :] = channel_rows(k_ref)
    for shift, part_ref in enumerate((w0_ref, w1_ref, w2_ref, w3_ref)):
        for z in range(4):
            part_ref[z] = w_ref[z * 4 + ((y_ref[0] + shift) & 3)]


def conv_kernel(xk_ref, o_ref, xpad, krow, tt, acc, ys):
    sort = one_hot(lambda r: ((r >> 2) & 31) * 16 + (r >> 7) * 4 + (r & 3), 512)

    def by_channel(rows):
        return jnp.dot(sort, rows, preferred_element_type=jnp.float32)

    xs_all = by_channel(xk_ref[:, :16, :].reshape(512, BLOCK))
    for c in range(NCH):
        xpad[c, :BLOCK, :] = jnp.zeros((BLOCK, BLOCK), jnp.float32)
        xpad[c, BLOCK:, :] = xs_all[c * BLOCK : (c + 1) * BLOCK, :]
    krow[...] = by_channel(xk_ref[:, 16:, :].reshape(512, BLOCK))
    upper = iota((BLOCK, BLOCK), 1) >= iota((BLOCK, BLOCK), 0)

    def channel(c, carry):
        before = jnp.zeros((BLOCK, BLOCK), jnp.float32)
        for first in range(0, BLOCK, CHUNK):
            pieces = []
            for j in range(CHUNK):
                m = first + j
                row = jnp.broadcast_to(krow[pl.ds(c * BLOCK + m, 1), :], (BLOCK, BLOCK))
                turned = pltpu.roll(row, 0, 1, stride=1, stride_axis=0)
                tt[j * BLOCK : (j + 1) * BLOCK, :] = jnp.where(upper, turned, before).astype(
                    jnp.bfloat16
                )
                before = turned
                pieces.append(
                    xpad[c, BLOCK - m + first : 2 * BLOCK - m, :].astype(jnp.bfloat16)
                )
            product = jnp.dot(
                jnp.concatenate(pieces, axis=1), tt[...], preferred_element_type=jnp.float32
            )
            if first == 0:
                acc[...] = product
            else:
                acc[first:, :] += product
        base = pl.multiple_of(c * BLOCK, BLOCK)
        ys[pl.ds(base, BLOCK), :] = acc[...].astype(jnp.bfloat16)
        return carry

    lax.fori_loop(0, NCH, channel, 0)
    back = one_hot(lambda r: ((r >> 2) & 3) * BLOCK + (r >> 4) * 4 + (r & 3), 512)
    spread = jnp.dot(back, ys[...], preferred_element_type=jnp.float32)
    o_ref[...] = spread.astype(jnp.bfloat16).reshape(32, 16, BLOCK)


def gate_kernel(y_ref, x_ref, g_ref, skip_ref, o_ref):
    rows = y_ref[...].reshape(512, BLOCK)
    source, channel = iota((512, BLOCK), 0), iota((512, BLOCK), 1)
    for b in range(4):
        pick = jnp.where(source == channel * 4 + b, 1.0, 0.0).astype(jnp.bfloat16)
        convolved = lax.dot_general(
            rows, pick, (((0,), (0,)), ((), ())), preferred_element_type=jnp.float32
        )
        span = slice(b * BLOCK, (b + 1) * BLOCK)
        v = g_ref[span, :].astype(jnp.float32)
        mixed = convolved + skip_ref[...] * x_ref[span, :].astype(jnp.float32)
        o_ref[span, :] = (mixed * (v / (1.0 + jnp.exp(-v)))).astype(jnp.bfloat16)


def mix_kernel(y_ref, g_ref, w0_ref, w1_ref, w2_ref, w3_ref, o_ref):
    gated = jnp.concatenate([g_ref[z] for z in range(4)], axis=1)
    for shift, w_ref in enumerate((w0_ref, w1_ref, w2_ref, w3_ref)):
        owner = (y_ref[0] + 4 - shift) & 3
        o_ref[owner] = jnp.dot(
            gated, w_ref[...].reshape(512, BLOCK), preferred_element_type=jnp.float32
        ).astype(jnp.bfloat16)


VMEM = pl.BlockSpec(memory_space=pltpu.VMEM)
SMEM = pl.BlockSpec(memory_space=pltpu.SMEM)


def shards(inputs, gate_in, kernel, skip_gain, out_weight):
    def out(*shape):
        return jax.ShapeDtypeStruct(shape, jnp.bfloat16)

    y = lax.axis_index("y").reshape(1)
    xk, w_own, *w_away = pl.pallas_call(
        prep_kernel,
        out_shape=(out(32, 32, BLOCK),) + (out(4, BLOCK, BLOCK),) * 4,
        in_specs=[SMEM] + [VMEM] * 3,
        out_specs=(VMEM,) * 5,
    )(y, inputs, kernel, out_weight.reshape(16, BLOCK, BLOCK))
    xk = lax.all_to_all(xk, CTX, 0, 0, tiled=True)
    w_parts = [w_own] + [
        lax.ppermute(w, "y", [(i, (i + shift) % 4) for i in range(4)])
        for shift, w in enumerate(w_away, 1)
    ]

    convolved = pl.pallas_call(
        conv_kernel,
        out_shape=out(32, 16, BLOCK),
        in_specs=[VMEM],
        out_specs=VMEM,
        scratch_shapes=[
            pltpu.VMEM((NCH, 2 * BLOCK, BLOCK), jnp.float32),
            pltpu.VMEM((512, BLOCK), jnp.float32),
            pltpu.VMEM((CHUNK * BLOCK, BLOCK), jnp.bfloat16),
            pltpu.VMEM((BLOCK, BLOCK), jnp.float32),
            pltpu.VMEM((512, BLOCK), jnp.bfloat16),
        ],
    )(xk)
    convolved = lax.all_to_all(convolved, CTX, 0, 0, tiled=True)

    gated = pl.pallas_call(
        gate_kernel, out_shape=out(512, BLOCK), in_specs=[VMEM] * 4, out_specs=VMEM
    )(convolved, inputs, gate_in, skip_gain.reshape(1, BLOCK))
    gated = lax.all_gather(gated, "zl")

    partial = pl.pallas_call(
        mix_kernel, out_shape=out(4, 512, BLOCK), in_specs=[SMEM] + [VMEM] * 5, out_specs=VMEM
    )(y, gated, *w_parts)
    partial = lax.all_to_all(partial, "y", 0, 0, tiled=True)
    return jnp.sum(partial.astype(jnp.float32), axis=0).astype(jnp.bfloat16)


def solution(mesh):
    fine = Mesh(mesh.devices.reshape(4, 4, 2, 4, 4), CTX + CH)
    placed = (P(CTX, CH), P(CTX, CH), P(CTX, CH), P(CH), P(None, CH))
    return jax.shard_map(
        shards, mesh=fine, in_specs=placed, out_specs=P(CTX, CH), check_vma=False
    )
```

```python
import math

import jax
import jax.numpy as jnp
import numpy as np
from jax import lax
from jax.experimental import pallas as pl
from jax.experimental.pallas import tpu as pltpu
from jax.sharding import Mesh, PartitionSpec as P

BLOCK = 128
CTX = ("zh", "x", "core")
CH = ("zl", "y")
NCH = 4


def two_parts(table):
    high = np.asarray(table, np.float32).astype(jnp.bfloat16)
    return high, (table - high.astype(np.float64)).astype(jnp.bfloat16)


def transform_tables():
    t, f = np.arange(2 * BLOCK)[:, None], np.arange(BLOCK)[None, :]
    angle = ((2 * f + 1) * t % (4 * BLOCK)) * (math.pi / (2 * BLOCK))
    cos, sin = np.cos(angle), np.sin(angle)
    inside_hi, inside_lo = two_parts(np.concatenate([cos[:BLOCK], -sin[:BLOCK]], axis=1))
    across_hi, across_lo = two_parts(np.concatenate([cos[:BLOCK].T, sin[:BLOCK].T], axis=0))
    return_hi, return_lo = two_parts(np.concatenate([cos[:BLOCK], sin[:BLOCK]], axis=1))
    out_hi, out_lo = two_parts(np.concatenate([cos.T, -sin.T], axis=0))
    return (
        np.concatenate([inside_hi, inside_lo], axis=0),
        np.concatenate([across_hi, across_hi, across_lo, across_lo], axis=1),
        np.concatenate([return_hi, return_hi, return_lo], axis=1),
        np.concatenate([out_hi, out_hi, out_lo], axis=0),
    )


def iota(shape, dim):
    return lax.broadcasted_iota(jnp.int32, shape, dim)


def dot(a, b):
    return jnp.dot(a, b, preferred_element_type=jnp.float32)


def split(value):
    high = value.astype(jnp.bfloat16)
    return high, (value - high.astype(jnp.float32)).astype(jnp.bfloat16)


def prep_kernel(x_ref, k_ref, xk_ref, turned, placed):
    for array, ref in enumerate((x_ref, k_ref)):
        for b in range(4):
            turned[b] = ref[b * BLOCK : (b + 1) * BLOCK, :].astype(jnp.float32).T
            for c in range(NCH):
                placed[array, pl.ds(b * 4 + c, 32, stride=16), :] = turned[
                    b, pl.ds(c, 32, stride=4), :
                ]
        xk_ref[:, array * 16 : array * 16 + 16, :] = (
            placed[array].astype(jnp.bfloat16).reshape(32, 16, BLOCK)
        )


def pick_kernel(y_ref, w_ref, w0_ref, w1_ref, w2_ref, w3_ref):
    for shift, part_ref in enumerate((w0_ref, w1_ref, w2_ref, w3_ref)):
        for z in range(4):
            part_ref[z] = w_ref[z * 4 + ((y_ref[0] + shift) & 3)]


def conv_kernel(
    xk_ref, inside_ref, across_ref, return_ref, out_ref, o_ref, xre, xim, kre, kim, late, ys
):
    for array, (re, im) in enumerate(((xre, xim), (kre, kim))):
        rows = xk_ref[:, array * 16 : array * 16 + 16, :].reshape(512, BLOCK)
        spectra = dot(jnp.concatenate([rows, rows], axis=1), inside_ref[...])
        re[...] = spectra[:, :BLOCK]
        im[...] = spectra[:, BLOCK:]
    late[:8, :] = jnp.zeros((8, BLOCK), jnp.float32)

    def across(re, im, mine):
        high, low = split(jnp.concatenate([re[mine, :], im[mine, :]], axis=1))
        mixed = dot(across_ref[...], jnp.concatenate([high, low, high, low], axis=0))
        cos_re, cos_im = mixed[:BLOCK, :BLOCK], mixed[:BLOCK, BLOCK:]
        sin_re, sin_im = mixed[BLOCK:, :BLOCK], mixed[BLOCK:, BLOCK:]
        return (cos_re + sin_im, cos_im - sin_re), (cos_re - sin_im, cos_im + sin_re)

    def times(p, q):
        return p[0] * q[0] - p[1] * q[1], p[0] * q[1] + p[1] * q[0]

    for c in range(NCH):
        mine = pl.ds(c, BLOCK, stride=4)
        x_up, x_down = across(xre, xim, mine)
        k_up, k_down = across(kre, kim, mine)
        up, down = times(x_up, k_up), times(x_down, k_down)
        both = jnp.concatenate(
            [
                jnp.concatenate([up[0] + down[0], up[1] + down[1]], axis=1),
                jnp.concatenate([down[1] - up[1], up[0] - down[0]], axis=1),
            ],
            axis=0,
        )
        high, low = split(both)
        blocks = dot(return_ref[...], jnp.concatenate([high, low, high], axis=0))
        high, low = split(blocks)
        rows = dot(jnp.concatenate([high, low, high], axis=1), out_ref[...])
        late[8:, :] = rows[:, BLOCK:]
        ys[mine, :] = (rows[:, :BLOCK] + late[7 : 7 + BLOCK, :]) * (1.0 / (256 * BLOCK))
    o_ref[...] = ys[...].astype(jnp.bfloat16).reshape(32, 16, BLOCK)


def gate_kernel(y_ref, x_ref, g_ref, skip_ref, o_ref):
    rows = y_ref[...].reshape(512, BLOCK)
    source, channel = iota((512, BLOCK), 0), iota((512, BLOCK), 1)
    for b in range(4):
        held = (channel >> 2) * 16 + b * 4 + (channel & 3)
        pick = jnp.where(source == held, 1.0, 0.0).astype(jnp.bfloat16)
        convolved = lax.dot_general(
            rows, pick, (((0,), (0,)), ((), ())), preferred_element_type=jnp.float32
        )
        span = slice(b * BLOCK, (b + 1) * BLOCK)
        v = g_ref[span, :].astype(jnp.float32)
        mixed = convolved + skip_ref[...] * x_ref[span, :].astype(jnp.float32)
        gated = (mixed * (v / (1.0 + jnp.exp(-v)))).astype(jnp.bfloat16)
        for z in range(4):
            o_ref[z, span, :] = gated


def mix_kernel(y_ref, g_ref, w0_ref, w1_ref, w2_ref, w3_ref, o_ref):
    gated = jnp.concatenate([g_ref[z] for z in range(4)], axis=1)
    for shift, w_ref in enumerate((w0_ref, w1_ref, w2_ref, w3_ref)):
        owner = (y_ref[0] + 4 - shift) & 3
        o_ref[owner] = jnp.dot(
            gated, w_ref[...].reshape(512, BLOCK), preferred_element_type=jnp.float32
        ).astype(jnp.bfloat16)


VMEM = pl.BlockSpec(memory_space=pltpu.VMEM)
SMEM = pl.BlockSpec(memory_space=pltpu.SMEM)


def near(array):
    return pltpu.with_memory_space_constraint(array, pltpu.VMEM)


def shards(inputs, gate_in, kernel, skip_gain, out_weight):
    def out(*shape):
        return jax.ShapeDtypeStruct(shape, jnp.bfloat16)

    def scratch(*shape):
        return pltpu.VMEM(shape, jnp.float32)

    y = lax.axis_index("y").reshape(1)
    xk = pl.pallas_call(
        prep_kernel,
        out_shape=out(32, 32, BLOCK),
        in_specs=[VMEM] * 2,
        out_specs=VMEM,
        scratch_shapes=[scratch(4, BLOCK, BLOCK), scratch(2, 512, BLOCK)],
    )(inputs, kernel)
    xk = near(lax.all_to_all(xk, CTX, 0, 0, tiled=True))
    w_own, *w_away = pl.pallas_call(
        pick_kernel,
        out_shape=(out(4, BLOCK, BLOCK),) * 4,
        in_specs=[SMEM, VMEM],
        out_specs=(VMEM,) * 4,
    )(y, out_weight.reshape(16, BLOCK, BLOCK))
    w_parts = [w_own] + [
        lax.ppermute(w, "y", [(i, (i + shift) % 4) for i in range(4)])
        for shift, w in enumerate(w_away, 1)
    ]

    tables = [near(jnp.asarray(table)) for table in transform_tables()]
    convolved = pl.pallas_call(
        conv_kernel,
        out_shape=out(32, 16, BLOCK),
        in_specs=[VMEM] * 5,
        out_specs=VMEM,
        scratch_shapes=[scratch(512, BLOCK)] * 4 + [scratch(8 + BLOCK, BLOCK), scratch(512, BLOCK)],
    )(xk, *tables)
    convolved = lax.all_to_all(convolved, CTX, 0, 0, tiled=True)
    convolved, *w_parts = lax.optimization_barrier((convolved, *w_parts))
    convolved, *w_parts = (near(array) for array in (convolved, *w_parts))

    gated = pl.pallas_call(
        gate_kernel, out_shape=out(4, 512, BLOCK), in_specs=[VMEM] * 4, out_specs=VMEM
    )(convolved, near(inputs), near(gate_in), skip_gain.reshape(1, BLOCK))
    gated = near(lax.all_to_all(gated, "zl", 0, 0, tiled=True))

    partial = pl.pallas_call(
        mix_kernel, out_shape=out(4, 512, BLOCK), in_specs=[SMEM] + [VMEM] * 5, out_specs=VMEM
    )(y, gated, *w_parts)
    partial = lax.all_to_all(partial, "y", 0, 0, tiled=True)
    return jnp.sum(partial.astype(jnp.float32), axis=0).astype(jnp.bfloat16)


def solution(mesh):
    fine = Mesh(mesh.devices.reshape(4, 4, 2, 4, 4), CTX + CH)
    placed = (P(CTX, CH), P(CTX, CH), P(CTX, CH), P(CH), P(None, CH))
    return jax.shard_map(
        shards, mesh=fine, in_specs=placed, out_specs=P(CTX, CH), check_vma=False
    )
```

```python
import math

import jax
import jax.numpy as jnp
import numpy as np
from jax import lax
from jax.experimental import pallas as pl
from jax.experimental.pallas import tpu as pltpu
from jax.sharding import Mesh, PartitionSpec as P

BLOCK = 128
CTX = ("zh", "x", "core")
CH = ("zl", "y")
NCH = 4


def two_parts(table):
    high = np.asarray(table, np.float32).astype(jnp.bfloat16)
    return high, (table - high.astype(np.float64)).astype(jnp.bfloat16)


def transform_tables():
    t, f = np.arange(2 * BLOCK)[:, None], np.arange(BLOCK)[None, :]
    angle = ((2 * f + 1) * t % (4 * BLOCK)) * (math.pi / (2 * BLOCK))
    cos, sin = np.cos(angle), np.sin(angle)
    inside_hi, inside_lo = two_parts(np.concatenate([cos[:BLOCK], -sin[:BLOCK]], axis=1))
    across_hi, across_lo = two_parts(np.concatenate([cos[:BLOCK].T, sin[:BLOCK].T], axis=0))
    return_hi, return_lo = two_parts(np.concatenate([cos[:BLOCK], sin[:BLOCK]], axis=1))
    out_hi, out_lo = two_parts(np.concatenate([cos.T, -sin.T], axis=0))
    return (
        np.concatenate([inside_hi, inside_lo], axis=0),
        np.concatenate([across_hi, across_hi, across_lo, across_lo], axis=1),
        np.concatenate([return_hi, return_hi, return_lo], axis=1),
        np.concatenate([out_hi, out_hi, out_lo], axis=0),
    )


def iota(shape, dim):
    return lax.broadcasted_iota(jnp.int32, shape, dim)


def dot(a, b):
    return jnp.dot(a, b, preferred_element_type=jnp.float32)


def split(value):
    high = value.astype(jnp.bfloat16)
    return high, (value - high.astype(jnp.float32)).astype(jnp.bfloat16)


def prep_kernel(x_ref, k_ref, xk_ref, turned, placed):
    for array, ref in enumerate((x_ref, k_ref)):
        for b in range(4):
            turned[b] = ref[b * BLOCK : (b + 1) * BLOCK, :].astype(jnp.float32).T
            for c in range(NCH):
                placed[array, pl.ds(b * 4 + c, 32, stride=16), :] = turned[
                    b, pl.ds(c, 32, stride=4), :
                ]
        xk_ref[:, array * 16 : array * 16 + 16, :] = (
            placed[array].astype(jnp.bfloat16).reshape(32, 16, BLOCK)
        )


def pick_kernel(y_ref, w_ref, w0_ref, w1_ref, w2_ref, w3_ref):
    for shift, part_ref in enumerate((w0_ref, w1_ref, w2_ref, w3_ref)):
        for z in range(4):
            part_ref[z] = w_ref[z * 4 + ((y_ref[0] + shift) & 3)]


def conv_kernel(
    xk_ref, inside_ref, across_ref, return_ref, out_ref, o_ref, xre, xim, kre, kim, late, ys
):
    for array, (re, im) in enumerate(((xre, xim), (kre, kim))):
        rows = xk_ref[:, array * 16 : array * 16 + 16, :].reshape(512, BLOCK)
        spectra = dot(jnp.concatenate([rows, rows], axis=1), inside_ref[...])
        re[...] = spectra[:, :BLOCK]
        im[...] = spectra[:, BLOCK:]
    late[:8, :] = jnp.zeros((8, BLOCK), jnp.float32)

    def across(re, im, mine):
        high, low = split(jnp.concatenate([re[mine, :], im[mine, :]], axis=1))
        mixed = dot(across_ref[...], jnp.concatenate([high, low, high, low], axis=0))
        cos_re, cos_im = mixed[:BLOCK, :BLOCK], mixed[:BLOCK, BLOCK:]
        sin_re, sin_im = mixed[BLOCK:, :BLOCK], mixed[BLOCK:, BLOCK:]
        return (cos_re + sin_im, cos_im - sin_re), (cos_re - sin_im, cos_im + sin_re)

    def times(p, q):
        return p[0] * q[0] - p[1] * q[1], p[0] * q[1] + p[1] * q[0]

    for c in range(NCH):
        mine = pl.ds(c, BLOCK, stride=4)
        x_up, x_down = across(xre, xim, mine)
        k_up, k_down = across(kre, kim, mine)
        up, down = times(x_up, k_up), times(x_down, k_down)
        both = jnp.concatenate(
            [
                jnp.concatenate([up[0] + down[0], up[1] + down[1]], axis=1),
                jnp.concatenate([down[1] - up[1], up[0] - down[0]], axis=1),
            ],
            axis=0,
        )
        high, low = split(both)
        blocks = dot(return_ref[...], jnp.concatenate([high, low, high], axis=0))
        high, low = split(blocks)
        rows = dot(jnp.concatenate([high, low, high], axis=1), out_ref[...])
        late[8:, :] = rows[:, BLOCK:]
        ys[mine, :] = (rows[:, :BLOCK] + late[7 : 7 + BLOCK, :]) * (1.0 / (256 * BLOCK))
    o_ref[...] = ys[...].astype(jnp.bfloat16).reshape(32, 16, BLOCK)


def gate_kernel(y_ref, x_ref, g_ref, skip_ref, o_ref):
    rows = y_ref[...].reshape(512, BLOCK)
    source, channel = iota((512, BLOCK), 0), iota((512, BLOCK), 1)
    for b in range(4):
        held = (channel >> 2) * 16 + b * 4 + (channel & 3)
        pick = jnp.where(source == held, 1.0, 0.0).astype(jnp.bfloat16)
        convolved = lax.dot_general(
            rows, pick, (((0,), (0,)), ((), ())), preferred_element_type=jnp.float32
        )
        span = slice(b * BLOCK, (b + 1) * BLOCK)
        v = g_ref[span, :].astype(jnp.float32)
        mixed = convolved + skip_ref[...] * x_ref[span, :].astype(jnp.float32)
        gated = (mixed * (v / (1.0 + jnp.exp(-v)))).astype(jnp.bfloat16)
        for z in range(4):
            o_ref[z, span, :] = gated


def mix_kernel(y_ref, g_ref, w0_ref, w1_ref, w2_ref, w3_ref, o_ref):
    gated = jnp.concatenate([g_ref[z] for z in range(4)], axis=1)
    for shift, w_ref in enumerate((w0_ref, w1_ref, w2_ref, w3_ref)):
        owner = (y_ref[0] + 4 - shift) & 3
        o_ref[owner] = jnp.dot(
            gated, w_ref[...].reshape(512, BLOCK), preferred_element_type=jnp.float32
        ).astype(jnp.bfloat16)


VMEM = pl.BlockSpec(memory_space=pltpu.VMEM)
SMEM = pl.BlockSpec(memory_space=pltpu.SMEM)


def near(array):
    return pltpu.with_memory_space_constraint(array, pltpu.VMEM)


def shards(inputs, gate_in, kernel, skip_gain, out_weight):
    def out(*shape):
        return pltpu.VMEM(shape, jnp.bfloat16)

    def scratch(*shape):
        return pltpu.VMEM(shape, jnp.float32)

    y = lax.axis_index("y").reshape(1)
    xk = pl.pallas_call(
        prep_kernel,
        out_shape=out(32, 32, BLOCK),
        in_specs=[VMEM] * 2,
        out_specs=VMEM,
        scratch_shapes=[scratch(4, BLOCK, BLOCK), scratch(2, 512, BLOCK)],
    )(inputs, kernel)
    xk = lax.all_to_all(xk, CTX, 0, 0, tiled=True)
    w_own, *w_away = pl.pallas_call(
        pick_kernel,
        out_shape=(out(4, BLOCK, BLOCK),) * 4,
        in_specs=[SMEM, VMEM],
        out_specs=(VMEM,) * 4,
    )(y, out_weight.reshape(16, BLOCK, BLOCK))
    w_parts = [w_own] + [
        lax.ppermute(w, "y", [(i, (i + shift) % 4) for i in range(4)])
        for shift, w in enumerate(w_away, 1)
    ]

    xk, *w_parts = lax.optimization_barrier((xk, *w_parts))
    xk, *w_parts = (near(array) for array in (xk, *w_parts))
    tables = [near(jnp.asarray(table)) for table in transform_tables()]
    convolved = pl.pallas_call(
        conv_kernel,
        out_shape=out(32, 16, BLOCK),
        in_specs=[VMEM] * 5,
        out_specs=VMEM,
        scratch_shapes=[scratch(512, BLOCK)] * 4 + [scratch(8 + BLOCK, BLOCK), scratch(512, BLOCK)],
    )(xk, *tables)
    convolved = near(lax.all_to_all(convolved, CTX, 0, 0, tiled=True))

    gated = pl.pallas_call(
        gate_kernel, out_shape=out(4, 512, BLOCK), in_specs=[VMEM] * 4, out_specs=VMEM
    )(convolved, near(inputs), near(gate_in), skip_gain.reshape(1, BLOCK))
    gated = near(lax.all_to_all(gated, "zl", 0, 0, tiled=True))

    partial = pl.pallas_call(
        mix_kernel, out_shape=out(4, 512, BLOCK), in_specs=[SMEM] + [VMEM] * 5, out_specs=VMEM
    )(y, gated, *w_parts)
    partial = lax.all_to_all(partial, "y", 0, 0, tiled=True)
    return jnp.sum(partial.astype(jnp.float32), axis=0).astype(jnp.bfloat16)


def solution(mesh):
    fine = Mesh(mesh.devices.reshape(4, 4, 2, 4, 4), CTX + CH)
    placed = (P(CTX, CH), P(CTX, CH), P(CTX, CH), P(CH), P(None, CH))
    return jax.shard_map(
        shards, mesh=fine, in_specs=placed, out_specs=P(CTX, CH), check_vma=False
    )
```

```python
import math

import jax
import jax.numpy as jnp
import numpy as np
from jax import lax
from jax.experimental import pallas as pl
from jax.experimental.pallas import tpu as pltpu
from jax.sharding import Mesh, PartitionSpec as P

BLOCK = 128
CTX = ("zh", "x", "core")
CH = ("zl", "y")
NCH = 4


def two_parts(table):
    high = np.asarray(table, np.float32).astype(jnp.bfloat16)
    return high, (table - high.astype(np.float64)).astype(jnp.bfloat16)


def transform_tables():
    t, f = np.arange(2 * BLOCK)[:, None], np.arange(BLOCK)[None, :]
    angle = ((2 * f + 1) * t % (4 * BLOCK)) * (math.pi / (2 * BLOCK))
    cos, sin = np.cos(angle), np.sin(angle)
    inside_hi, inside_lo = two_parts(np.concatenate([cos[:BLOCK], -sin[:BLOCK]], axis=1))
    across_hi, across_lo = two_parts(np.concatenate([cos[:BLOCK].T, sin[:BLOCK].T], axis=0))
    return_hi, return_lo = two_parts(np.concatenate([cos[:BLOCK], sin[:BLOCK]], axis=1))
    out_hi, out_lo = two_parts(np.concatenate([cos.T, -sin.T], axis=0))
    return (
        np.concatenate([inside_hi, inside_lo], axis=0),
        np.concatenate([across_hi, across_hi, across_lo, across_lo], axis=1),
        np.concatenate([return_hi, return_hi, return_lo], axis=1),
        np.concatenate([out_hi, out_hi, out_lo], axis=0),
    )


def iota(shape, dim):
    return lax.broadcasted_iota(jnp.int32, shape, dim)


def dot(a, b):
    return jnp.dot(a, b, preferred_element_type=jnp.float32)


def split(value):
    high = value.astype(jnp.bfloat16)
    return high, (value - high.astype(jnp.float32)).astype(jnp.bfloat16)


def prep_kernel(x_ref, k_ref, xk_ref, turned, placed):
    for array, ref in enumerate((x_ref, k_ref)):
        for b in range(4):
            turned[b] = ref[b * BLOCK : (b + 1) * BLOCK, :].astype(jnp.float32).T
            for c in range(NCH):
                placed[array, pl.ds(b * 4 + c, 32, stride=16), :] = turned[
                    b, pl.ds(c, 32, stride=4), :
                ]
        xk_ref[:, array * 16 : array * 16 + 16, :] = (
            placed[array].astype(jnp.bfloat16).reshape(32, 16, BLOCK)
        )


def pick_kernel(y_ref, w_ref, w0_ref, w1_ref, w2_ref, w3_ref):
    for shift, part_ref in enumerate((w0_ref, w1_ref, w2_ref, w3_ref)):
        for z in range(4):
            part_ref[z] = w_ref[z * 4 + ((y_ref[0] + shift) & 3)]


def conv_kernel(
    xk_ref, inside_ref, across_ref, return_ref, out_ref, o_ref, xre, xim, kre, kim, mixed, blocks, late, ys
):
    for array, (re, im) in enumerate(((xre, xim), (kre, kim))):
        rows = xk_ref[:, array * 16 : array * 16 + 16, :].reshape(512, BLOCK)
        spectra = dot(jnp.concatenate([rows, rows], axis=1), inside_ref[...])
        re[...] = spectra[:, :BLOCK]
        im[...] = spectra[:, BLOCK:]

    def across(re, im, mine):
        high, low = split(jnp.concatenate([re[mine, :], im[mine, :]], axis=1))
        both = dot(across_ref[...], jnp.concatenate([high, low, high, low], axis=0))
        cos_re, cos_im = both[:BLOCK, :BLOCK], both[:BLOCK, BLOCK:]
        sin_re, sin_im = both[BLOCK:, :BLOCK], both[BLOCK:, BLOCK:]
        return (cos_re + sin_im, cos_im - sin_re), (cos_re - sin_im, cos_im + sin_re)

    def times(p, q):
        return p[0] * q[0] - p[1] * q[1], p[0] * q[1] + p[1] * q[0]

    def keep(ref, c, rows, columns, value):
        high, low = split(value)
        ref[c, rows, columns] = high
        ref[c, rows.start + 2 * BLOCK : rows.stop + 2 * BLOCK, columns] = low
        ref[c, rows.start + 4 * BLOCK : rows.stop + 4 * BLOCK, columns] = high

    first, second = slice(0, BLOCK), slice(BLOCK, 2 * BLOCK)
    for c in range(NCH):
        mine = pl.ds(c, BLOCK, stride=4)
        x_up, x_down = across(xre, xim, mine)
        k_up, k_down = across(kre, kim, mine)
        up, down = times(x_up, k_up), times(x_down, k_down)
        keep(mixed, c, first, first, up[0] + down[0])
        keep(mixed, c, first, second, up[1] + down[1])
        keep(mixed, c, second, first, down[1] - up[1])
        keep(mixed, c, second, second, up[0] - down[0])
    for c in range(NCH):
        high, low = split(dot(return_ref[...], mixed[c]))
        blocks[c, :, :256] = high
        blocks[c, :, 256:512] = low
        blocks[c, :, 512:] = high
    for c in range(NCH):
        rows = dot(blocks[c], out_ref[...])
        late[c, :8, :] = jnp.zeros((8, BLOCK), jnp.float32)
        late[c, 8:, :] = rows[:, BLOCK:]
        ys[pl.ds(c, BLOCK, stride=4), :] = (rows[:, :BLOCK] + late[c, 7 : 7 + BLOCK, :]) * (
            1.0 / (256 * BLOCK)
        )
    o_ref[...] = ys[...].astype(jnp.bfloat16).reshape(32, 16, BLOCK)


def gate_kernel(y_ref, x_ref, g_ref, skip_ref, o_ref):
    rows = y_ref[...].reshape(512, BLOCK)
    source, channel = iota((512, BLOCK), 0), iota((512, BLOCK), 1)
    for b in range(4):
        held = (channel >> 2) * 16 + b * 4 + (channel & 3)
        pick = jnp.where(source == held, 1.0, 0.0).astype(jnp.bfloat16)
        convolved = lax.dot_general(
            rows, pick, (((0,), (0,)), ((), ())), preferred_element_type=jnp.float32
        )
        span = slice(b * BLOCK, (b + 1) * BLOCK)
        v = g_ref[span, :].astype(jnp.float32)
        mixed = convolved + skip_ref[...] * x_ref[span, :].astype(jnp.float32)
        gated = (mixed * (v / (1.0 + jnp.exp(-v)))).astype(jnp.bfloat16)
        o_ref[span, :] = gated


def mix_kernel(y_ref, g_ref, w0_ref, w1_ref, w2_ref, w3_ref, o_ref):
    gated = jnp.concatenate([g_ref[z] for z in range(4)], axis=1)
    for shift, w_ref in enumerate((w0_ref, w1_ref, w2_ref, w3_ref)):
        owner = (y_ref[0] + 4 - shift) & 3
        o_ref[owner] = jnp.dot(
            gated, w_ref[...].reshape(512, BLOCK), preferred_element_type=jnp.float32
        ).astype(jnp.bfloat16)


VMEM = pl.BlockSpec(memory_space=pltpu.VMEM)
SMEM = pl.BlockSpec(memory_space=pltpu.SMEM)


def near(array):
    return pltpu.with_memory_space_constraint(array, pltpu.VMEM)


def shards(inputs, gate_in, kernel, skip_gain, out_weight):
    def out(*shape):
        return pltpu.VMEM(shape, jnp.bfloat16)

    def scratch(*shape):
        return pltpu.VMEM(shape, jnp.float32)

    y = lax.axis_index("y").reshape(1)
    xk = pl.pallas_call(
        prep_kernel,
        out_shape=out(32, 32, BLOCK),
        in_specs=[VMEM] * 2,
        out_specs=VMEM,
        scratch_shapes=[scratch(4, BLOCK, BLOCK), scratch(2, 512, BLOCK)],
    )(inputs, kernel)
    xk = near(lax.all_to_all(xk, CTX, 0, 0, tiled=True))
    w_own, *w_away = pl.pallas_call(
        pick_kernel,
        out_shape=(out(4, BLOCK, BLOCK),) * 4,
        in_specs=[SMEM, VMEM],
        out_specs=(VMEM,) * 4,
    )(y, out_weight.reshape(16, BLOCK, BLOCK))
    w_parts = [w_own] + [
        lax.ppermute(w, "y", [(i, (i + shift) % 4) for i in range(4)])
        for shift, w in enumerate(w_away, 1)
    ]

    tables = [near(jnp.asarray(table)) for table in transform_tables()]
    convolved = pl.pallas_call(
        conv_kernel,
        out_shape=out(32, 16, BLOCK),
        in_specs=[VMEM] * 5,
        out_specs=VMEM,
        scratch_shapes=[scratch(512, BLOCK)] * 4
        + [out(NCH, 6 * BLOCK, 2 * BLOCK), out(NCH, BLOCK, 6 * BLOCK)]
        + [scratch(NCH, 8 + BLOCK, BLOCK), scratch(512, BLOCK)],
    )(xk, *tables)
    convolved = near(lax.all_to_all(convolved, CTX, 0, 0, tiled=True))
    w_parts = [near(array) for array in w_parts]

    gated = pl.pallas_call(
        gate_kernel, out_shape=out(512, BLOCK), in_specs=[VMEM] * 4, out_specs=VMEM
    )(convolved, near(inputs), near(gate_in), skip_gain.reshape(1, BLOCK))
    gated = near(lax.all_gather(gated, "zl"))

    partial = pl.pallas_call(
        mix_kernel, out_shape=out(4, 512, BLOCK), in_specs=[SMEM] + [VMEM] * 5, out_specs=VMEM
    )(y, gated, *w_parts)
    partial = lax.all_to_all(partial, "y", 0, 0, tiled=True)
    return jnp.sum(partial.astype(jnp.float32), axis=0).astype(jnp.bfloat16)


def solution(mesh):
    fine = Mesh(mesh.devices.reshape(4, 4, 2, 4, 4), CTX + CH)
    placed = (P(CTX, CH), P(CTX, CH), P(CTX, CH), P(CH), P(None, CH))
    return jax.shard_map(
        shards, mesh=fine, in_specs=placed, out_specs=P(CTX, CH), check_vma=False
    )
```

```python
import math

import jax
import jax.numpy as jnp
import numpy as np
from jax import lax
from jax.experimental import pallas as pl
from jax.experimental.pallas import tpu as pltpu
from jax.sharding import Mesh, PartitionSpec as P

BLOCK = 128
CTX = ("zh", "x", "core")
CH = ("zl", "y")
NCH = 4


def two_parts(table):
    high = np.asarray(table, np.float32).astype(jnp.bfloat16)
    return high, (table - high.astype(np.float64)).astype(jnp.bfloat16)


def transform_tables():
    t, f = np.arange(2 * BLOCK)[:, None], np.arange(BLOCK)[None, :]
    angle = ((2 * f + 1) * t % (4 * BLOCK)) * (math.pi / (2 * BLOCK))
    cos, sin = np.cos(angle), np.sin(angle)
    inside_hi, inside_lo = two_parts(np.concatenate([cos[:BLOCK], -sin[:BLOCK]], axis=1))
    across_hi, across_lo = two_parts(np.concatenate([cos[:BLOCK].T, sin[:BLOCK].T], axis=0))
    return_hi, return_lo = two_parts(np.concatenate([cos[:BLOCK], sin[:BLOCK]], axis=1))
    out_hi, out_lo = two_parts(np.concatenate([cos.T, -sin.T], axis=0))
    return (
        np.concatenate([inside_hi, inside_lo], axis=0),
        np.concatenate([across_hi, across_hi, across_lo], axis=1),
        np.concatenate([return_hi, return_hi, return_lo], axis=1),
        np.concatenate([out_hi, out_hi, out_lo], axis=0),
    )


def iota(shape, dim):
    return lax.broadcasted_iota(jnp.int32, shape, dim)


def dot(a, b):
    return jnp.dot(a, b, preferred_element_type=jnp.float32)


def split(value):
    high = value.astype(jnp.bfloat16)
    return high, (value - high.astype(jnp.float32)).astype(jnp.bfloat16)


def prep_kernel(x_ref, k_ref, xk_ref, placed):
    for array, ref in enumerate((x_ref, k_ref)):
        for b in range(4):
            turned = ref[b * BLOCK : (b + 1) * BLOCK, :].astype(jnp.float32).T
            for c in range(NCH):
                placed[array, pl.ds(b * 4 + c, 32, stride=16), :] = turned[c * 32 : c * 32 + 32, :]
        xk_ref[:, array * 16 : array * 16 + 16, :] = (
            placed[array].astype(jnp.bfloat16).reshape(32, 16, BLOCK)
        )


def pick_kernel(w_ref, w0_ref, w1_ref, w2_ref, w3_ref):
    for shift, part_ref in enumerate((w0_ref, w1_ref, w2_ref, w3_ref)):
        for z in range(4):
            part_ref[z] = w_ref[z * 4 + ((lax.axis_index("y") + shift) & 3)]


def conv_kernel(
    xk_ref, inside_ref, across_ref, return_ref, out_ref, o_ref, xre, xim, kre, kim, mixed, blocks, late, ys
):
    for array, (re, im) in enumerate(((xre, xim), (kre, kim))):
        rows = xk_ref[:, array * 16 : array * 16 + 16, :].reshape(512, BLOCK)
        spectra = dot(jnp.concatenate([rows, rows], axis=1), inside_ref[...])
        re[...] = spectra[:, :BLOCK]
        im[...] = spectra[:, BLOCK:]

    def across(re, im, mine):
        high, low = split(jnp.concatenate([re[mine, :], im[mine, :]], axis=1))
        both = dot(across_ref[...], jnp.concatenate([high, low, high], axis=0))
        cos_re, cos_im = both[:BLOCK, :BLOCK], both[:BLOCK, BLOCK:]
        sin_re, sin_im = both[BLOCK:, :BLOCK], both[BLOCK:, BLOCK:]
        return (cos_re + sin_im, cos_im - sin_re), (cos_re - sin_im, cos_im + sin_re)

    def times(p, q):
        return p[0] * q[0] - p[1] * q[1], p[0] * q[1] + p[1] * q[0]

    def keep(ref, c, rows, columns, value):
        high, low = split(value)
        ref[c, rows, columns] = high
        ref[c, rows.start + 2 * BLOCK : rows.stop + 2 * BLOCK, columns] = low
        ref[c, rows.start + 4 * BLOCK : rows.stop + 4 * BLOCK, columns] = high

    first, second = slice(0, BLOCK), slice(BLOCK, 2 * BLOCK)
    for c in range(NCH):
        mine = pl.ds(c, BLOCK, stride=4)
        x_up, x_down = across(xre, xim, mine)
        k_up, k_down = across(kre, kim, mine)
        up, down = times(x_up, k_up), times(x_down, k_down)
        keep(mixed, c, first, first, up[0] + down[0])
        keep(mixed, c, first, second, up[1] + down[1])
        keep(mixed, c, second, first, down[1] - up[1])
        keep(mixed, c, second, second, up[0] - down[0])
    for c in range(NCH):
        high, low = split(dot(return_ref[...], mixed[c]))
        blocks[c * BLOCK : (c + 1) * BLOCK, :256] = high
        blocks[c * BLOCK : (c + 1) * BLOCK, 256:512] = low
        blocks[c * BLOCK : (c + 1) * BLOCK, 512:] = high
    for c in range(NCH):
        rows = dot(blocks[c * BLOCK : (c + 1) * BLOCK, :], out_ref[...])
        late[c, :8, :] = jnp.zeros((8, BLOCK), jnp.float32)
        late[c, 8:, :] = rows[:, BLOCK:]
        ys[pl.ds(c, BLOCK, stride=4), :] = (rows[:, :BLOCK] + late[c, 7 : 7 + BLOCK, :]) * (
            1.0 / (256 * BLOCK)
        )
    o_ref[...] = ys[...].astype(jnp.bfloat16).reshape(32, 16, BLOCK)


def gate_kernel(y_ref, x_ref, g_ref, skip_ref, o_ref):
    rows = y_ref[...].reshape(512, BLOCK)
    source, channel = iota((512, BLOCK), 0), iota((512, BLOCK), 1)
    for b in range(4):
        held = (channel & 31) * 16 + b * 4 + (channel >> 5)
        pick = jnp.where(source == held, 1.0, 0.0).astype(jnp.bfloat16)
        convolved = lax.dot_general(
            rows, pick, (((0,), (0,)), ((), ())), preferred_element_type=jnp.float32
        )
        span = slice(b * BLOCK, (b + 1) * BLOCK)
        v = g_ref[span, :].astype(jnp.float32)
        mixed = convolved + skip_ref[...] * x_ref[span, :].astype(jnp.float32)
        gated = (mixed * (v / (1.0 + jnp.exp(-v)))).astype(jnp.bfloat16)
        o_ref[span, :] = gated


def mix_kernel(g_ref, w0_ref, w1_ref, w2_ref, w3_ref, o_ref):
    gated = jnp.concatenate([g_ref[z] for z in range(4)], axis=1)
    for shift, w_ref in enumerate((w0_ref, w1_ref, w2_ref, w3_ref)):
        owner = (lax.axis_index("y") + 4 - shift) & 3
        o_ref[owner] = jnp.dot(
            gated, w_ref[...].reshape(512, BLOCK), preferred_element_type=jnp.float32
        ).astype(jnp.bfloat16)


VMEM = pl.BlockSpec(memory_space=pltpu.VMEM)


def near(array):
    return pltpu.with_memory_space_constraint(array, pltpu.VMEM)


def shards(inputs, gate_in, kernel, skip_gain, out_weight):
    def out(*shape):
        return pltpu.VMEM(shape, jnp.bfloat16)

    def scratch(*shape):
        return pltpu.VMEM(shape, jnp.float32)

    xk = pl.pallas_call(
        prep_kernel,
        out_shape=out(32, 32, BLOCK),
        in_specs=[VMEM] * 2,
        out_specs=VMEM,
        scratch_shapes=[scratch(2, 512, BLOCK)],
    )(inputs, kernel)
    xk = near(lax.all_to_all(xk, CTX, 0, 0, tiled=True))
    w_own, *w_away = pl.pallas_call(
        pick_kernel,
        out_shape=(out(4, BLOCK, BLOCK),) * 4,
        in_specs=[VMEM],
        out_specs=(VMEM,) * 4,
    )(out_weight.reshape(16, BLOCK, BLOCK))
    w_parts = [w_own] + [
        lax.ppermute(w, "y", [(i, (i + shift) % 4) for i in range(4)])
        for shift, w in enumerate(w_away, 1)
    ]

    tables = [near(jnp.asarray(table)) for table in transform_tables()]
    convolved = pl.pallas_call(
        conv_kernel,
        out_shape=out(32, 16, BLOCK),
        in_specs=[VMEM] * 5,
        out_specs=VMEM,
        scratch_shapes=[scratch(512, BLOCK)] * 4
        + [out(NCH, 6 * BLOCK, 2 * BLOCK), out(512, 6 * BLOCK)]
        + [scratch(NCH, 8 + BLOCK, BLOCK), scratch(512, BLOCK)],
    )(xk, *tables)
    convolved = near(lax.all_to_all(convolved, CTX, 0, 0, tiled=True))
    w_parts = [near(array) for array in w_parts]

    gated = pl.pallas_call(
        gate_kernel, out_shape=out(512, BLOCK), in_specs=[VMEM] * 4, out_specs=VMEM
    )(convolved, near(inputs), near(gate_in), near(skip_gain.reshape(1, BLOCK)))
    gated = near(lax.all_gather(gated, "zl"))

    partial = pl.pallas_call(
        mix_kernel, out_shape=out(4, 512, BLOCK), in_specs=[VMEM] * 5, out_specs=VMEM
    )(gated, *w_parts)
    partial = lax.all_to_all(partial, "y", 0, 0, tiled=True)
    return jnp.sum(partial.astype(jnp.float32), axis=0).astype(jnp.bfloat16)


def solution(mesh):
    fine = Mesh(mesh.devices.reshape(4, 4, 2, 4, 4), CTX + CH)
    placed = (P(CTX, CH), P(CTX, CH), P(CTX, CH), P(CH), P(None, CH))
    return jax.shard_map(
        shards, mesh=fine, in_specs=placed, out_specs=P(CTX, CH), check_vma=False
    )
```

```python
import math

import jax
import jax.numpy as jnp
import numpy as np
from jax import lax
from jax.experimental import pallas as pl
from jax.experimental.pallas import tpu as pltpu
from jax.sharding import Mesh, PartitionSpec as P

BLOCK = 128
CTX = ("zh", "x", "core")
CH = ("zl", "y")
PEERS = ("core", "x", "zh")
SIZE = {"zh": 4, "x": 4, "core": 2}
NCH = 4


def ctx_of_peers():
    places = np.arange(32).reshape([SIZE[axis] for axis in CTX])
    return places.transpose([CTX.index(axis) for axis in PEERS]).reshape(-1)


def two_parts(table):
    high = np.asarray(table, np.float32).astype(jnp.bfloat16)
    return high, (table - high.astype(np.float64)).astype(jnp.bfloat16)


def transform_tables():
    t, f = np.arange(2 * BLOCK)[:, None], np.arange(BLOCK)[None, :]
    angle = ((2 * f + 1) * t % (4 * BLOCK)) * (math.pi / (2 * BLOCK))
    cos, sin = np.cos(angle), np.sin(angle)
    inside_hi, inside_lo = two_parts(np.concatenate([cos[:BLOCK], -sin[:BLOCK]], axis=1))
    held = (ctx_of_peers()[:, None] * 4 + np.arange(4)).reshape(-1)
    across_hi, across_lo = two_parts(np.concatenate([cos[held].T, sin[held].T], axis=0))
    return_hi, return_lo = two_parts(np.concatenate([cos[:BLOCK], sin[:BLOCK]], axis=1))
    out_hi, out_lo = two_parts(np.concatenate([cos.T, -sin.T], axis=0))
    return (
        np.concatenate([inside_hi, inside_lo], axis=0),
        np.concatenate([across_hi, across_hi, across_lo], axis=1),
        np.concatenate([return_hi, return_hi, return_lo], axis=1),
        np.concatenate([out_hi, out_hi, out_lo], axis=0),
    )


def iota(shape, dim):
    return lax.broadcasted_iota(jnp.int32, shape, dim)


def dot(a, b):
    return jnp.dot(a, b, preferred_element_type=jnp.float32)


def split(value):
    high = value.astype(jnp.bfloat16)
    return high, (value - high.astype(jnp.float32)).astype(jnp.bfloat16)


def prep_kernel(x_ref, k_ref, xk_ref, placed):
    for array, ref in enumerate((x_ref, k_ref)):
        for b in range(4):
            turned = ref[b * BLOCK : (b + 1) * BLOCK, :].astype(jnp.float32).T
            for c in range(NCH):
                placed[array, pl.ds(b * 4 + c, 32, stride=16), :] = turned[c * 32 : c * 32 + 32, :]
        xk_ref[:, array * 16 : array * 16 + 16, :] = (
            placed[array].astype(jnp.bfloat16).reshape(32, 16, BLOCK)
        )


def pick_kernel(w_ref, w0_ref, w1_ref, w2_ref, w3_ref):
    for shift, part_ref in enumerate((w0_ref, w1_ref, w2_ref, w3_ref)):
        for z in range(4):
            part_ref[z] = w_ref[z * 4 + ((lax.axis_index("y") + shift) & 3)]


def conv_kernel(
    xk_ref, inside_ref, across_ref, return_ref, out_ref, o_ref, xre, xim, kre, kim, mixed, blocks, late, ys
):
    for array, (re, im) in enumerate(((xre, xim), (kre, kim))):
        rows = xk_ref[:, array * 16 : array * 16 + 16, :].reshape(512, BLOCK)
        spectra = dot(jnp.concatenate([rows, rows], axis=1), inside_ref[...])
        re[...] = spectra[:, :BLOCK]
        im[...] = spectra[:, BLOCK:]

    def across(re, im, mine):
        high, low = split(jnp.concatenate([re[mine, :], im[mine, :]], axis=1))
        both = dot(across_ref[...], jnp.concatenate([high, low, high], axis=0))
        cos_re, cos_im = both[:BLOCK, :BLOCK], both[:BLOCK, BLOCK:]
        sin_re, sin_im = both[BLOCK:, :BLOCK], both[BLOCK:, BLOCK:]
        return (cos_re + sin_im, cos_im - sin_re), (cos_re - sin_im, cos_im + sin_re)

    def times(p, q):
        return p[0] * q[0] - p[1] * q[1], p[0] * q[1] + p[1] * q[0]

    def keep(ref, c, rows, columns, value):
        high, low = split(value)
        ref[c, rows, columns] = high
        ref[c, rows.start + 2 * BLOCK : rows.stop + 2 * BLOCK, columns] = low
        ref[c, rows.start + 4 * BLOCK : rows.stop + 4 * BLOCK, columns] = high

    first, second = slice(0, BLOCK), slice(BLOCK, 2 * BLOCK)
    for c in range(NCH):
        mine = pl.ds(c, BLOCK, stride=4)
        x_up, x_down = across(xre, xim, mine)
        k_up, k_down = across(kre, kim, mine)
        up, down = times(x_up, k_up), times(x_down, k_down)
        keep(mixed, c, first, first, up[0] + down[0])
        keep(mixed, c, first, second, up[1] + down[1])
        keep(mixed, c, second, first, down[1] - up[1])
        keep(mixed, c, second, second, up[0] - down[0])
    for c in range(NCH):
        high, low = split(dot(return_ref[...], mixed[c]))
        blocks[c * BLOCK : (c + 1) * BLOCK, :256] = high
        blocks[c * BLOCK : (c + 1) * BLOCK, 256:512] = low
        blocks[c * BLOCK : (c + 1) * BLOCK, 512:] = high
    for c in range(NCH):
        rows = dot(blocks[c * BLOCK : (c + 1) * BLOCK, :], out_ref[...])
        late[c, :8, :] = jnp.zeros((8, BLOCK), jnp.float32)
        late[c, 8:, :] = rows[:, BLOCK:]
        ys[pl.ds(c, BLOCK, stride=4), :] = (rows[:, :BLOCK] + late[c, 7 : 7 + BLOCK, :]) * (
            1.0 / (256 * BLOCK)
        )
    for peer, place in enumerate(ctx_of_peers().tolist()):
        o_ref[peer] = ys[place * 16 : place * 16 + 16, :].astype(jnp.bfloat16)


def gate_kernel(y_ref, x_ref, g_ref, skip_ref, o_ref):
    rows = y_ref[...].reshape(512, BLOCK)
    source, channel = iota((512, BLOCK), 0), iota((512, BLOCK), 1)
    for b in range(4):
        held = (channel & 31) * 16 + b * 4 + (channel >> 5)
        pick = jnp.where(source == held, 1.0, 0.0).astype(jnp.bfloat16)
        convolved = lax.dot_general(
            rows, pick, (((0,), (0,)), ((), ())), preferred_element_type=jnp.float32
        )
        span = slice(b * BLOCK, (b + 1) * BLOCK)
        v = g_ref[span, :].astype(jnp.float32)
        mixed = convolved + skip_ref[...] * x_ref[span, :].astype(jnp.float32)
        gated = (mixed * (v / (1.0 + jnp.exp(-v)))).astype(jnp.bfloat16)
        o_ref[span, :] = gated


def mix_kernel(g_ref, w0_ref, w1_ref, w2_ref, w3_ref, o_ref):
    gated = jnp.concatenate([g_ref[z] for z in range(4)], axis=1)
    for shift, w_ref in enumerate((w0_ref, w1_ref, w2_ref, w3_ref)):
        owner = (lax.axis_index("y") + 4 - shift) & 3
        o_ref[owner] = jnp.dot(
            gated, w_ref[...].reshape(512, BLOCK), preferred_element_type=jnp.float32
        ).astype(jnp.bfloat16)


VMEM = pl.BlockSpec(memory_space=pltpu.VMEM)


def near(array):
    return pltpu.with_memory_space_constraint(array, pltpu.VMEM)


def shards(inputs, gate_in, kernel, skip_gain, out_weight):
    def out(*shape):
        return pltpu.VMEM(shape, jnp.bfloat16)

    def scratch(*shape):
        return pltpu.VMEM(shape, jnp.float32)

    xk = pl.pallas_call(
        prep_kernel,
        out_shape=out(32, 32, BLOCK),
        in_specs=[VMEM] * 2,
        out_specs=VMEM,
        scratch_shapes=[scratch(2, 512, BLOCK)],
    )(inputs, kernel)
    xk = near(lax.all_to_all(xk, PEERS, 0, 0, tiled=True))
    w_own, *w_away = pl.pallas_call(
        pick_kernel,
        out_shape=(out(4, BLOCK, BLOCK),) * 4,
        in_specs=[VMEM],
        out_specs=(VMEM,) * 4,
    )(out_weight.reshape(16, BLOCK, BLOCK))
    w_parts = [w_own] + [
        lax.ppermute(w, "y", [(i, (i + shift) % 4) for i in range(4)])
        for shift, w in enumerate(w_away, 1)
    ]

    tables = [near(jnp.asarray(table)) for table in transform_tables()]
    convolved = pl.pallas_call(
        conv_kernel,
        out_shape=out(32, 16, BLOCK),
        in_specs=[VMEM] * 5,
        out_specs=VMEM,
        scratch_shapes=[scratch(512, BLOCK)] * 4
        + [out(NCH, 6 * BLOCK, 2 * BLOCK), out(512, 6 * BLOCK)]
        + [scratch(NCH, 8 + BLOCK, BLOCK), scratch(512, BLOCK)],
    )(xk, *tables)
    convolved = near(lax.all_to_all(convolved, PEERS, 0, 0, tiled=True))
    w_parts = [near(array) for array in w_parts]

    gated = pl.pallas_call(
        gate_kernel, out_shape=out(512, BLOCK), in_specs=[VMEM] * 4, out_specs=VMEM
    )(convolved, near(inputs), near(gate_in), near(skip_gain.reshape(1, BLOCK)))
    gated = near(lax.all_gather(gated, "zl"))

    partial = pl.pallas_call(
        mix_kernel, out_shape=out(4, 512, BLOCK), in_specs=[VMEM] * 5, out_specs=VMEM
    )(gated, *w_parts)
    partial = lax.all_to_all(partial, "y", 0, 0, tiled=True)
    return jnp.sum(partial.astype(jnp.float32), axis=0).astype(jnp.bfloat16)


def solution(mesh):
    fine = Mesh(mesh.devices.reshape(4, 4, 2, 4, 4), CTX + CH)
    placed = (P(CTX, CH), P(CTX, CH), P(CTX, CH), P(CH), P(None, CH))
    return jax.shard_map(
        shards, mesh=fine, in_specs=placed, out_specs=P(CTX, CH), check_vma=False
    )
```

```python
import math

import jax
import jax.numpy as jnp
import numpy as np
from jax import lax
from jax.experimental import pallas as pl
from jax.experimental.pallas import tpu as pltpu
from jax.sharding import Mesh, PartitionSpec as P

BLOCK = 128
CTX = ("zh", "x", "core")
CH = ("zl", "y")
PEERS = ("x", "zh", "core")
SIZE = {"zh": 4, "x": 4, "core": 2}
NCH = 4


def ctx_of_peers():
    places = np.arange(32).reshape([SIZE[axis] for axis in CTX])
    return places.transpose([CTX.index(axis) for axis in PEERS]).reshape(-1)


def two_parts(table):
    high = np.asarray(table, np.float32).astype(jnp.bfloat16)
    return high, (table - high.astype(np.float64)).astype(jnp.bfloat16)


def transform_tables():
    t, f = np.arange(2 * BLOCK)[:, None], np.arange(BLOCK)[None, :]
    angle = ((2 * f + 1) * t % (4 * BLOCK)) * (math.pi / (2 * BLOCK))
    cos, sin = np.cos(angle), np.sin(angle)
    inside_hi, inside_lo = two_parts(np.concatenate([cos[:BLOCK], -sin[:BLOCK]], axis=1))
    held = (ctx_of_peers()[:, None] * 4 + np.arange(4)).reshape(-1)
    across_hi, across_lo = two_parts(np.concatenate([cos[held].T, sin[held].T], axis=0))
    return_hi, return_lo = two_parts(np.concatenate([cos[:BLOCK], sin[:BLOCK]], axis=1))
    out_hi, out_lo = two_parts(np.concatenate([cos.T, -sin.T], axis=0))
    return (
        np.concatenate([inside_hi, inside_lo], axis=0),
        np.concatenate([across_hi, across_hi, across_lo], axis=1),
        np.concatenate([return_hi, return_hi, return_lo], axis=1),
        np.concatenate([out_hi, out_hi, out_lo], axis=0),
    )


def iota(shape, dim):
    return lax.broadcasted_iota(jnp.int32, shape, dim)


def dot(a, b):
    return jnp.dot(a, b, preferred_element_type=jnp.float32)


def split(value):
    high = value.astype(jnp.bfloat16)
    return high, (value - high.astype(jnp.float32)).astype(jnp.bfloat16)


def prep_kernel(x_ref, k_ref, xk_ref, placed):
    for array, ref in enumerate((x_ref, k_ref)):
        for b in range(4):
            turned = ref[b * BLOCK : (b + 1) * BLOCK, :].astype(jnp.float32).T
            for c in range(NCH):
                placed[array, pl.ds(b * 4 + c, 32, stride=16), :] = turned[c * 32 : c * 32 + 32, :]
        xk_ref[:, array * 16 : array * 16 + 16, :] = (
            placed[array].astype(jnp.bfloat16).reshape(32, 16, BLOCK)
        )


def pick_kernel(w_ref, w0_ref, w1_ref, w2_ref, w3_ref):
    for shift, part_ref in enumerate((w0_ref, w1_ref, w2_ref, w3_ref)):
        for z in range(4):
            part_ref[z] = w_ref[z * 4 + ((lax.axis_index("y") + shift) & 3)]


def conv_kernel(
    xk_ref, inside_ref, across_ref, return_ref, out_ref, o_ref, xre, xim, kre, kim, mixed, blocks, late, ys
):
    for array, (re, im) in enumerate(((xre, xim), (kre, kim))):
        rows = xk_ref[:, array * 16 : array * 16 + 16, :].reshape(512, BLOCK)
        spectra = dot(jnp.concatenate([rows, rows], axis=1), inside_ref[...])
        re[...] = spectra[:, :BLOCK]
        im[...] = spectra[:, BLOCK:]

    def across(re, im, mine):
        high, low = split(jnp.concatenate([re[mine, :], im[mine, :]], axis=1))
        both = dot(across_ref[...], jnp.concatenate([high, low, high], axis=0))
        cos_re, cos_im = both[:BLOCK, :BLOCK], both[:BLOCK, BLOCK:]
        sin_re, sin_im = both[BLOCK:, :BLOCK], both[BLOCK:, BLOCK:]
        return (cos_re + sin_im, cos_im - sin_re), (cos_re - sin_im, cos_im + sin_re)

    def times(p, q):
        return p[0] * q[0] - p[1] * q[1], p[0] * q[1] + p[1] * q[0]

    def keep(ref, c, rows, columns, value):
        high, low = split(value)
        ref[c, rows, columns] = high
        ref[c, rows.start + 2 * BLOCK : rows.stop + 2 * BLOCK, columns] = low
        ref[c, rows.start + 4 * BLOCK : rows.stop + 4 * BLOCK, columns] = high

    first, second = slice(0, BLOCK), slice(BLOCK, 2 * BLOCK)
    for c in range(NCH):
        mine = pl.ds(c, BLOCK, stride=4)
        x_up, x_down = across(xre, xim, mine)
        k_up, k_down = across(kre, kim, mine)
        up, down = times(x_up, k_up), times(x_down, k_down)
        keep(mixed, c, first, first, up[0] + down[0])
        keep(mixed, c, first, second, up[1] + down[1])
        keep(mixed, c, second, first, down[1] - up[1])
        keep(mixed, c, second, second, up[0] - down[0])
    for c in range(NCH):
        high, low = split(dot(return_ref[...], mixed[c]))
        blocks[c * BLOCK : (c + 1) * BLOCK, :256] = high
        blocks[c * BLOCK : (c + 1) * BLOCK, 256:512] = low
        blocks[c * BLOCK : (c + 1) * BLOCK, 512:] = high
    for c in range(NCH):
        rows = dot(blocks[c * BLOCK : (c + 1) * BLOCK, :], out_ref[...])
        late[c, :8, :] = jnp.zeros((8, BLOCK), jnp.float32)
        late[c, 8:, :] = rows[:, BLOCK:]
        ys[pl.ds(c, BLOCK, stride=4), :] = (rows[:, :BLOCK] + late[c, 7 : 7 + BLOCK, :]) * (
            1.0 / (256 * BLOCK)
        )
    for peer, place in enumerate(ctx_of_peers().tolist()):
        o_ref[peer] = ys[place * 16 : place * 16 + 16, :].astype(jnp.bfloat16)


def gate_kernel(y_ref, x_ref, g_ref, skip_ref, o_ref):
    rows = y_ref[...].reshape(512, BLOCK)
    source, channel = iota((512, BLOCK), 0), iota((512, BLOCK), 1)
    for b in range(4):
        held = (channel & 31) * 16 + b * 4 + (channel >> 5)
        pick = jnp.where(source == held, 1.0, 0.0).astype(jnp.bfloat16)
        convolved = lax.dot_general(
            rows, pick, (((0,), (0,)), ((), ())), preferred_element_type=jnp.float32
        )
        span = slice(b * BLOCK, (b + 1) * BLOCK)
        v = g_ref[span, :].astype(jnp.float32)
        mixed = convolved + skip_ref[...] * x_ref[span, :].astype(jnp.float32)
        gated = (mixed * (v / (1.0 + jnp.exp(-v)))).astype(jnp.bfloat16)
        o_ref[span, :] = gated


def mix_kernel(g_ref, w0_ref, w1_ref, w2_ref, w3_ref, o_ref):
    gated = jnp.concatenate([g_ref[z] for z in range(4)], axis=1)
    for shift, w_ref in enumerate((w0_ref, w1_ref, w2_ref, w3_ref)):
        owner = (lax.axis_index("y") + 4 - shift) & 3
        o_ref[owner] = jnp.dot(
            gated, w_ref[...].reshape(512, BLOCK), preferred_element_type=jnp.float32
        ).astype(jnp.bfloat16)


VMEM = pl.BlockSpec(memory_space=pltpu.VMEM)


def near(array):
    return pltpu.with_memory_space_constraint(array, pltpu.VMEM)


def shards(inputs, gate_in, kernel, skip_gain, out_weight):
    def out(*shape):
        return pltpu.VMEM(shape, jnp.bfloat16)

    def scratch(*shape):
        return pltpu.VMEM(shape, jnp.float32)

    xk = pl.pallas_call(
        prep_kernel,
        out_shape=out(32, 32, BLOCK),
        in_specs=[VMEM] * 2,
        out_specs=VMEM,
        scratch_shapes=[scratch(2, 512, BLOCK)],
    )(inputs, kernel)
    xk = near(lax.all_to_all(xk, PEERS, 0, 0, tiled=True))
    w_own, *w_away = pl.pallas_call(
        pick_kernel,
        out_shape=(out(4, BLOCK, BLOCK),) * 4,
        in_specs=[VMEM],
        out_specs=(VMEM,) * 4,
    )(out_weight.reshape(16, BLOCK, BLOCK))
    w_parts = [w_own] + [
        lax.ppermute(w, "y", [(i, (i + shift) % 4) for i in range(4)])
        for shift, w in enumerate(w_away, 1)
    ]

    tables = [near(jnp.asarray(table)) for table in transform_tables()]
    convolved = pl.pallas_call(
        conv_kernel,
        out_shape=out(32, 16, BLOCK),
        in_specs=[VMEM] * 5,
        out_specs=VMEM,
        scratch_shapes=[scratch(512, BLOCK)] * 4
        + [out(NCH, 6 * BLOCK, 2 * BLOCK), out(512, 6 * BLOCK)]
        + [scratch(NCH, 8 + BLOCK, BLOCK), scratch(512, BLOCK)],
    )(xk, *tables)
    convolved = near(lax.all_to_all(convolved, PEERS, 0, 0, tiled=True))
    w_parts = [near(array) for array in w_parts]

    gated = pl.pallas_call(
        gate_kernel, out_shape=out(512, BLOCK), in_specs=[VMEM] * 4, out_specs=VMEM
    )(convolved, near(inputs), near(gate_in), near(skip_gain.reshape(1, BLOCK)))
    gated = near(lax.all_gather(gated, "zl"))

    partial = pl.pallas_call(
        mix_kernel, out_shape=out(4, 512, BLOCK), in_specs=[VMEM] * 5, out_specs=VMEM
    )(gated, *w_parts)
    partial = lax.all_to_all(partial, "y", 0, 0, tiled=True)
    return jnp.sum(partial.astype(jnp.float32), axis=0).astype(jnp.bfloat16)


def solution(mesh):
    fine = Mesh(mesh.devices.reshape(4, 4, 2, 4, 4), CTX + CH)
    placed = (P(CTX, CH), P(CTX, CH), P(CTX, CH), P(CH), P(None, CH))
    return jax.shard_map(
        shards, mesh=fine, in_specs=placed, out_specs=P(CTX, CH), check_vma=False
    )
```
